512 devices in a mesh: ctx: 16 (over y, z_lo), exp: 32 (over z_hi, x, core).
Axes of the slice: x: 4, y: 4, z: 16 (z_hi: 4, z_lo: 4; z = z_hi * 4 + z_lo), core: 2. Of those that a mesh axis runs over, the one named last changes fastest.
Arguments:
- query: bfloat16 [32, 1024, 2048], P('exp', 'ctx'), may hold values from -24 to 24
- key_value: bfloat16 [32, 1024, 2, 256], P('exp', 'ctx'), may hold values from -24 to 24
- positions: int32 [32, 1024], P('exp', 'ctx'), may hold values from 0 to 1023, as said below
- resid: bfloat16 [32, 1024, 1440], P('exp', 'ctx'), may hold values from -6 to 6
- sinks: float32 [32], replicated, may hold values from -2 to 3
- o_weight: bfloat16 [2048, 1440], P('exp'), may hold values from -0.125 to 0.125
- norm_gain: float32 [1440], replicated, may hold values from 0.25 to 1.75
- expert_ids: int32 [32, 1024, 4], P('exp', 'ctx'), may hold values from 0 to 127, all different within a row; in each aligned block of 64 rows (0 to 63, 64 to 127, ..., all dimensions but the last counted through in order) at most 2 rows name the same one
- route_weights: float32 [32, 1024, 4], P('exp', 'ctx'), may hold values from 0.1 to 0.5
- w_gate: bfloat16 [1440, 184320], P(None, ('ctx', 'exp')), may hold values from -0.15625 to 0.15625
- w_up: bfloat16 [1440, 184320], P(None, ('ctx', 'exp')), may hold values from -0.15625 to 0.15625
- w_down: bfloat16 [184320, 1440], P(('ctx', 'exp')), may hold values from -0.15625 to 0.15625
Outputs:
- out: bfloat16 [32, 1024, 1440], P('exp', 'ctx')
The draws below stay inside these ranges and needn't reach their ends.
Inputs may be any that keep to these rules, and one draw needn't show every extreme that they name: Within each sequence every position appears once; the 64 stored rows of one device are two runs of 32 consecutive ascending positions, each run starting at a multiple of 32. `expert_ids`: each row names 4 different experts; among the 64 rows of one device no expert is named more than 2 times, a bound that some block reaches.
All inputs are finite; a program needn't handle non-finite values.
Results may differ from the reference program's by a relative error of at most 0.0075.
Values may be sent and summed in bfloat16 or wider, within the bound.
No kernel may reach another device: no remote copies, remote signals or barrier semaphores. Data moves between devices by JAX's collectives and lax.ppermute only.
A program may use at most 64 MiB of HBM per device.

```python
import math
import jax
import jax.numpy as jnp
import numpy as np
from jax import lax

D = 1440
QH = 32
KVH = 4
HD = 64
FF_E = 1440
TOP = 4
SLICES = 4
TOK_DEV = 64
SEQS = 32
LENGTH = 1024
HALF = 32
EXPERTS = 128
CAP = 2
N_CTX = 16
N_EXP = 32


def draw_query(key, part):
    shape = (SEQS, LENGTH, QH * HD)
    noise = jnp.clip(jax.random.normal(jax.random.fold_in(key, 1), shape, jnp.float32), -6.0, 6.0)
    return noise.astype(jnp.bfloat16)


def draw_key_value(key, part):
    shape = (SEQS, LENGTH, 2, KVH * HD)
    values = jnp.clip(jax.random.normal(jax.random.fold_in(key, 2), shape, jnp.float32), -6.0, 6.0)
    return values.astype(jnp.bfloat16)


def draw_positions(key, part):
    blocks = LENGTH // HALF
    keys = jax.random.split(jax.random.fold_in(key, 3), SEQS)
    order = jax.vmap(lambda single: jax.random.permutation(single, blocks))(keys)
    spread = order[:, :, None] * HALF + jnp.arange(HALF)[None, None, :]
    return spread.reshape(SEQS, LENGTH).astype(jnp.int32)


def shard_levels(stream_key, extent, cuts, low, largest):
    factor_of, own = 1.0, jax.random.fold_in(stream_key, 6)
    for position, blocks in cuts:
        heights = jnp.exp(jax.random.uniform(jax.random.fold_in(own, position), (blocks,), jnp.float32, low / len(cuts), largest / len(cuts)))
        factor_of = factor_of * jnp.repeat(heights, extent[position] // blocks).reshape([-1 if axis == position else 1 for axis in range(len(extent))])
    return factor_of


def deal_out(stream_key, own, number, rows, amount, top, most, lean):
    sequence = jax.random.permutation(stream_key, amount)
    crowded, common = portions_of(amount, rows * top, most, lean, True), portions_of(amount, rows * top, most, lean, False)
    places = jnp.arange(amount)

    def named(lengths, turn):
        used = int((lengths > 0).sum())
        fixed = max(1, used // 4)
        passed = fixed + (places - fixed + turn * (used - fixed)) % max(1, amount - fixed)
        return jnp.zeros((amount,), jnp.int32).at[sequence[jnp.where(places < fixed, places, passed)]].set(jnp.asarray(lengths, jnp.int32))

    lengths = jnp.where(number % 4 == 0, named(crowded, number // 4), named(common, number - number // 4 - 1))
    mixed = jax.random.permutation(jax.random.fold_in(own, 3), amount)
    source_of, receiver = mixed[0:amount // 2 * 2:2], mixed[1:amount // 2 * 2:2]
    room = jnp.minimum(lengths[source_of] - 1, most - lengths[receiver]) // 2
    room = jnp.where((source_of == sequence[0]) | (receiver == sequence[0]) | (lengths[receiver] == 0), 0, jnp.maximum(room, 0))
    passed = jax.random.randint(jax.random.fold_in(own, 4), (amount // 2,), 0, 1 << 20) % (room + 1)
    lengths = lengths.at[source_of].add(-passed).at[receiver].add(passed)
    items = jnp.searchsorted(jnp.cumsum(lengths), jnp.arange(rows * top), side="right").astype(jnp.int32)
    table = items.reshape(top, rows).T
    table = table[jax.random.permutation(jax.random.fold_in(own, 1), rows)]
    turn = jax.random.randint(jax.random.fold_in(own, 2), (rows, 1), 0, top)
    return jnp.take_along_axis(table, (jnp.arange(top)[None, :] + turn) % top, axis=1)


def portions_of(amount, total, most, skew, full):
    loads = [(1 << 20) // math.isqrt(grade ** skew) + 1 for grade in range(1, amount + 1)]
    largest = most if full else min(most, max(-(-total // amount), total * loads[0] // sum(loads)))
    least = 1 if total - largest >= amount - 1 else 0
    given, rest = [largest] + [least] * (amount - 1), total - largest - least * (amount - 1)
    while rest > 0:
        candidates = [i for i in range(1, amount) if given[i] < largest] or [i for i in range(1, amount) if given[i] < most]
        pool, budget = sum([loads[i] for i in candidates]), rest
        for i in candidates:
            addition = min(most - given[i], max(1, budget * loads[i] // pool), rest)
            given[i] = given[i] + addition
            rest = rest - addition
    return np.array(given)


def scatter_about(stream_key, dims, deviation, bound, cuts=(), held_as=jnp.bfloat16):
    factor_of = shard_levels(stream_key, dims, cuts, -0.22, 0.18) if cuts else 1.0
    drawn = jax.random.normal(stream_key, dims, jnp.float32) * deviation * factor_of
    return jnp.minimum(jnp.maximum(drawn, -bound), bound).astype(held_as)


def setup_inputs(seed: int = 0) -> dict:
    splits = jax.random.split(jax.random.key(seed), 13)
    query = draw_query(jax.random.fold_in(splits[12], 71), 0)
    key_value = draw_key_value(jax.random.fold_in(splits[12], 71), 0)
    positions = draw_positions(jax.random.fold_in(splits[12], 71), 0)
    resid = scatter_about(splits[3], (SEQS, LENGTH, D), 1.0, 6.0, ((0, 32), (1, 16)))
    sinks = jnp.clip(jax.random.uniform(splits[4], (QH,), jnp.float32, -2.0, 3.0), -2.0, 3.0)
    o_weight = scatter_about(splits[5], (QH * HD, D), (QH * HD) ** -0.5, 0.125, ((0, 32),))
    norm_gain = jnp.clip(1.0 + 0.15 * jax.random.normal(splits[6], (D,), jnp.float32), 0.25, 1.75)
    expert_ids_keys = jax.random.split(jax.random.fold_in(splits[7], 1), SEQS * LENGTH // TOK_DEV)
    expert_ids_turns = jax.random.permutation(jax.random.fold_in(splits[7], 3), SEQS * LENGTH // TOK_DEV)
    expert_ids = jax.vmap(lambda own, number: deal_out(jax.random.fold_in(splits[7], 2), own, number, TOK_DEV, EXPERTS, TOP, CAP, 2))(expert_ids_keys, expert_ids_turns).reshape((SEQS, LENGTH, TOP))
    route_weights = jnp.clip(0.1 + 0.4 * jax.random.uniform(splits[8], (SEQS, LENGTH, TOP), jnp.float32) ** shard_levels(splits[8], (SEQS, LENGTH, TOP), ((0, 32), (1, 16)), -0.2, 0.2), 0.1, 0.5)
    w_gate = scatter_about(splits[9], (D, EXPERTS * FF_E), D ** -0.5, 0.15625, ((1, 512),))
    w_up = scatter_about(splits[10], (D, EXPERTS * FF_E), D ** -0.5, 0.15625, ((1, 512),))
    w_down = scatter_about(splits[11], (EXPERTS * FF_E, D), FF_E ** -0.5, 0.15625, ((0, 512),))
    return {"query": query, "key_value": key_value, "positions": positions, "resid": resid, "sinks": sinks, "o_weight": o_weight, "norm_gain": norm_gain, "expert_ids": expert_ids, "route_weights": route_weights, "w_gate": w_gate, "w_up": w_up, "w_down": w_down}


NEG_FILL = -1e+30

def sequence_attention(query, key_value, positions, sinks):
    length = query.shape[0]
    group = QH // KVH
    grouped = query.reshape(length, KVH, group, HD).astype(jnp.float32)
    keys = key_value[:, 0].reshape(length, KVH, HD).astype(jnp.float32)
    values = key_value[:, 1].reshape(length, KVH, HD).astype(jnp.float32)
    scores = jnp.einsum('qgjd,kgd->gjqk', grouped, keys, precision=lax.Precision.HIGHEST) * (1.0 / math.sqrt(HD))
    allowed = positions[None, :] <= positions[:, None]
    scores = jnp.where(allowed[None, None], scores, NEG_FILL)
    sink = sinks.reshape(KVH, group)[:, :, None]
    top = jnp.maximum(lax.optimization_barrier(jnp.max(scores, axis=-1)), sink)
    weights = jnp.exp(scores - top[..., None])
    total = lax.optimization_barrier(jnp.sum(weights, axis=-1)) + jnp.exp(sink - top)
    mixed = jnp.einsum('gjqk,kgd->gjqd', weights, values, precision=lax.Precision.HIGHEST) / total[..., None]
    mixed = jnp.transpose(mixed, (2, 0, 1, 3))
    return mixed.reshape(length, QH * HD).astype(jnp.bfloat16)

def reference(query, key_value, positions, resid, sinks, o_weight, norm_gain, expert_ids, route_weights, w_gate, w_up, w_down):
    attended = lax.map(lambda items: sequence_attention(items[0], items[1], items[2], sinks), (query, key_value, positions))
    tokens = SEQS * LENGTH
    attended = attended.reshape(tokens, QH * HD)
    mixed = resid.reshape(tokens, D).astype(jnp.float32) + jnp.dot(attended, o_weight, preferred_element_type=jnp.float32)
    normed = (mixed * lax.rsqrt(lax.optimization_barrier(jnp.mean(mixed * mixed, axis=-1, keepdims=True)) + 1e-05) * norm_gain).astype(jnp.bfloat16)
    n_choices = tokens * TOP
    most_rows = N_CTX * N_EXP * CAP
    flat_ids = expert_ids.reshape(n_choices).astype(jnp.int32)
    order = jnp.argsort(flat_ids, stable=True).astype(jnp.int32)
    counts = jnp.bincount(flat_ids, length=EXPERTS).astype(jnp.int32)
    starts = (jnp.cumsum(counts) - counts).astype(jnp.int32)
    sorted_rows = normed[order // TOP]
    padded = jnp.concatenate([sorted_rows, jnp.zeros((most_rows, D), jnp.bfloat16)], axis=0)
    width = FF_E // SLICES

    def one_expert(carry, expert):
        start = starts[expert]
        block = lax.dynamic_slice_in_dim(padded, start, most_rows, 0)
        gate = jnp.dot(block, lax.dynamic_slice_in_dim(w_gate, expert * FF_E, FF_E, 1), preferred_element_type=jnp.float32)
        lifted = jnp.dot(block, lax.dynamic_slice_in_dim(w_up, expert * FF_E, FF_E, 1), preferred_element_type=jnp.float32)
        active = (gate * jax.nn.sigmoid(1.702 * gate) * (lifted + 1.0)).astype(jnp.bfloat16)
        down = lax.dynamic_slice_in_dim(w_down, expert * FF_E, FF_E, 0)
        partials = jnp.einsum('msf,sfd->smd', active.reshape(most_rows, SLICES, width).astype(jnp.float32), down.reshape(SLICES, width, D).astype(jnp.float32), precision=lax.Precision.HIGHEST).astype(jnp.bfloat16)
        result = lax.optimization_barrier(jnp.sum(partials.astype(jnp.float32), axis=0)).astype(jnp.bfloat16)
        valid = jnp.arange(most_rows, dtype=jnp.int32) < counts[expert]
        result = jnp.where(valid[:, None], result, jnp.zeros((), jnp.bfloat16))
        current = lax.dynamic_slice_in_dim(carry, start, most_rows, 0)
        carry = lax.dynamic_update_slice_in_dim(carry, current + result, start, 0)
        return (carry, None)
    initial = jnp.zeros((n_choices + most_rows, D), jnp.bfloat16)
    collected, _ = lax.scan(one_expert, initial, jnp.arange(EXPERTS, dtype=jnp.int32))
    expert_out = jnp.zeros((n_choices, D), jnp.bfloat16).at[order].set(collected[:n_choices])
    expert_out = expert_out.reshape(tokens, TOP, D).astype(jnp.float32)
    final = mixed + lax.optimization_barrier(jnp.sum(route_weights.reshape(tokens, TOP, 1) * expert_out, axis=1))
    return final.astype(jnp.bfloat16).reshape(SEQS, LENGTH, D)
```

```python
import functools
import math

import jax
import jax.numpy as jnp
from jax import lax
from jax.experimental import pallas as pl
from jax.experimental.pallas import tpu as pltpu
from jax.sharding import PartitionSpec as P

D = 1440
QH = 32
KVH = 4
HD = 64
TOP = 4
SLICES = 4
RUN = 32
EXPERTS = 128
LOG2E = math.log2(math.e)
NEG = -1e30
F32 = jnp.float32
BF16 = jnp.bfloat16


def attend_kernel(qpos_ref, sinks_ref, q_ref, kv_ref, out_ref, q_sc, k_sc, v_sc, bias_sc):
    rows = q_ref.shape[0]
    shards = kv_ref.shape[0]
    length = shards * rows
    group = QH // KVH
    for head in range(QH):
        q_sc[head // 2, (head % 2) * rows : (head % 2 + 1) * rows, :] = q_ref[
            :, head * HD : (head + 1) * HD
        ]
    kv = kv_ref[:, 0:rows, :].reshape(length, 2 * KVH * HD)
    ones = jnp.ones((length, HD), BF16)
    for g in range(KVH):
        k_sc[g] = kv[:, g * HD : (g + 1) * HD]
        v_sc[g] = jnp.concatenate(
            [kv[:, (KVH + g) * HD : (KVH + g + 1) * HD], ones], axis=1
        )
    number = jnp.concatenate([kv_ref[s, rows : rows + 1, 0:rows] for s in range(shards)], axis=1)
    lane = lax.broadcasted_iota(jnp.int32, (1, length), 1)
    key_pos = number.astype(F32).astype(jnp.int32) * RUN + lane % RUN
    bias = jnp.where(key_pos <= qpos_ref[...], 0.0, NEG).astype(F32)
    bias_sc[0:rows] = bias
    bias_sc[rows : 2 * rows] = bias
    pairs = group // 2

    def step(i, carry):
        g = i // pairs
        scores = lax.dot_general(
            q_sc[i], k_sc[g], (((1,), (1,)), ((), ())), preferred_element_type=F32
        )
        scores = scores * (LOG2E / math.sqrt(HD)) + bias_sc[...]
        row = lax.broadcasted_iota(jnp.int32, (2 * rows, 1), 0)
        sink = jnp.where(row < rows, sinks_ref[2 * i], sinks_ref[2 * i + 1]) * LOG2E
        top = jnp.maximum(jnp.max(scores, axis=1, keepdims=True), sink)
        weights = jnp.exp2(scores - top).astype(BF16)
        mixed = jnp.dot(weights, v_sc[g], preferred_element_type=F32)
        total = mixed[:, HD : HD + 1] + jnp.exp2(sink - top)
        result = (mixed[:, 0:HD] / total).astype(BF16)
        out_ref[:, pl.ds(pl.multiple_of(i * 2 * HD, 2 * HD), 2 * HD)] = jnp.concatenate(
            [result[0:rows], result[rows : 2 * rows]], axis=1
        )
        return carry

    lax.fori_loop(0, QH // 2, step, 0)


def attend(query, gathered, query_pos, sinks):
    rows = query.shape[0]
    shards = gathered.shape[0]
    length = shards * rows
    vmem = pl.BlockSpec(memory_space=pltpu.VMEM)
    return pl.pallas_call(
        attend_kernel,
        out_shape=jax.ShapeDtypeStruct((rows, QH * HD), BF16),
        in_specs=[vmem, pl.BlockSpec(memory_space=pltpu.SMEM), vmem, vmem],
        out_specs=vmem,
        scratch_shapes=[
            pltpu.VMEM((QH // 2, 2 * rows, HD), BF16),
            pltpu.VMEM((KVH, length, HD), BF16),
            pltpu.VMEM((KVH, length, 2 * HD), BF16),
            pltpu.VMEM((2 * rows, length), F32),
        ],
        compiler_params=pltpu.CompilerParams(vmem_limit_bytes=24 << 20),
        name="attend",
    )(query_pos[:, None], sinks, query, gathered)


def named(ids_ref, rank_cols):
    rows = ids_ref.shape[0]
    expert = lax.broadcasted_iota(jnp.int32, (rows, EXPERTS), 1)
    hits = [ids_ref[:, k : k + 1] == expert for k in range(TOP)]
    any_hit = functools.reduce(jnp.logical_or, hits)
    mask = any_hit.astype(F32)
    before = (
        lax.broadcasted_iota(jnp.int32, (rows, rows), 1)
        < lax.broadcasted_iota(jnp.int32, (rows, rows), 0)
    ).astype(F32)
    earlier = jnp.dot(
        before.astype(BF16), mask.astype(BF16), preferred_element_type=F32
    )
    first = mask * (earlier < 0.5).astype(F32)
    second = mask - first
    return hits, first, second


def project_kernel(att_ref, ow_ref, resid_ref, gain_ref, ids_ref, mixed_ref, out_ref, acc):
    @pl.when(pl.program_id(0) == 0)
    def _():
        acc[...] = resid_ref[...].astype(F32)

    acc[...] += jnp.dot(att_ref[...], ow_ref[...], preferred_element_type=F32)

    @pl.when(pl.program_id(0) == pl.num_programs(0) - 1)
    def _():
        mixed = acc[...]
        mixed_ref[...] = mixed
        scale = lax.rsqrt(jnp.mean(mixed * mixed, axis=1, keepdims=True) + 1e-05)
        normed = (mixed * scale * gain_ref[...]).astype(BF16)
        _, first, second = named(ids_ref, None)
        chosen = jnp.concatenate([first, second], axis=1).astype(BF16)
        out_ref[...] = lax.dot_general(
            chosen, normed, (((0,), (0,)), ((), ())), preferred_element_type=F32
        ).astype(BF16)


def project(attended, o_weight, resid, gain, ids):
    rows = attended.shape[0]
    depth = o_weight.shape[0]
    tile = 512
    whole = lambda i: (0, 0)
    return pl.pallas_call(
        project_kernel,
        grid=(depth // tile,),
        out_shape=(
            jax.ShapeDtypeStruct((rows, D), F32),
            jax.ShapeDtypeStruct((rows * TOP, D), BF16),
        ),
        in_specs=[
            pl.BlockSpec((rows, tile), lambda i: (0, i)),
            pl.BlockSpec((tile, D), lambda i: (i, 0)),
            pl.BlockSpec((rows, D), whole),
            pl.BlockSpec((1, D), whole),
            pl.BlockSpec((rows, TOP), whole),
        ],
        out_specs=(pl.BlockSpec((rows, D), whole), pl.BlockSpec((rows * TOP, D), whole)),
        scratch_shapes=[pltpu.VMEM((rows, D), F32)],
        compiler_params=pltpu.CompilerParams(vmem_limit_bytes=24 << 20),
        name="project",
    )(attended, o_weight, resid, gain[None, :], ids)


def experts_kernel(x_ref, *refs):
    n = 3 * SLICES
    weights, out_ref = refs[:n], refs[n]
    held, sems = refs[n + 1 : 2 * n + 1], refs[2 * n + 1]
    copies = [
        pltpu.make_async_copy(weights[i], held[i], sems.at[i]) for i in range(n)
    ]
    for copy in copies:
        copy.start()
    x = x_ref[...]
    total = None
    for s in range(SLICES):
        copies[3 * s].wait()
        gate = jnp.dot(x, held[3 * s][...], preferred_element_type=F32)
        copies[3 * s + 1].wait()
        up = jnp.dot(x, held[3 * s + 1][...], preferred_element_type=F32)
        active = (gate * jax.nn.sigmoid(1.702 * gate) * (up + 1.0)).astype(BF16)
        copies[3 * s + 2].wait()
        part = jnp.dot(active, held[3 * s + 2][...], preferred_element_type=F32)
        total = part if total is None else total + part
    out_ref[...] = total.astype(BF16)


def experts(x, weights):
    vmem = pl.BlockSpec(memory_space=pltpu.VMEM)
    return pl.pallas_call(
        experts_kernel,
        out_shape=jax.ShapeDtypeStruct(x.shape, BF16),
        in_specs=[vmem] + [pl.BlockSpec(memory_space=pl.ANY)] * len(weights),
        out_specs=vmem,
        scratch_shapes=[pltpu.VMEM(w.shape, w.dtype) for w in weights]
        + [pltpu.SemaphoreType.DMA((len(weights),))],
        compiler_params=pltpu.CompilerParams(vmem_limit_bytes=28 << 20),
        name="experts",
    )(x, *weights)


def combine_kernel(ids_ref, rw_ref, mixed_ref, back_ref, out_ref):
    hits, first, second = named(ids_ref, None)
    share = sum(
        jnp.where(hits[k], rw_ref[:, k : k + 1], 0.0) for k in range(TOP)
    )
    both = jnp.concatenate([share * first, share * second], axis=1)
    high = both.astype(BF16)
    low = (both - high.astype(F32)).astype(BF16)
    back = back_ref[...]
    out_ref[...] = (
        mixed_ref[...]
        + jnp.dot(high, back, preferred_element_type=F32)
        + jnp.dot(low, back, preferred_element_type=F32)
    ).astype(BF16)


def combine(ids, shares, mixed, back):
    vmem = pl.BlockSpec(memory_space=pltpu.VMEM)
    return pl.pallas_call(
        combine_kernel,
        out_shape=jax.ShapeDtypeStruct(mixed.shape, BF16),
        in_specs=[vmem] * 4,
        out_specs=vmem,
        compiler_params=pltpu.CompilerParams(vmem_limit_bytes=16 << 20),
        name="combine",
    )(ids, shares, mixed, back)


def swapped(value, bit):
    n = lax.axis_size("exp")
    return lax.ppermute(value, "exp", [(i, i ^ bit) for i in range(n)])


def body(
    query,
    key_value,
    positions,
    resid,
    sinks,
    o_weight,
    norm_gain,
    expert_ids,
    route_weights,
    w_gate,
    w_up,
    w_down,
):
    n_ctx, n_exp = lax.axis_size("ctx"), lax.axis_size("exp")
    rows = query.shape[1]
    pos = positions[0]
    numbers = jnp.broadcast_to((pos // RUN).astype(BF16)[None, :], (8, rows))
    own = jnp.concatenate(
        [
            key_value[0].reshape(rows, 2 * KVH * HD),
            jnp.pad(numbers, ((0, 0), (0, 2 * KVH * HD - rows))),
        ],
        axis=0,
    )
    gathered = lax.all_to_all(
        jnp.broadcast_to(own[None], (n_ctx,) + own.shape), "ctx", 0, 0, tiled=True
    )
    mine = (w_gate, w_up, w_down)
    beside = tuple(swapped(w, 2) for w in mine)
    core = tuple(swapped(w, 1) for w in mine)
    core_beside = tuple(swapped(w, 1) for w in beside)
    all_o = lax.all_gather(o_weight, "exp", axis=0, tiled=True)

    attended = attend(query[0], gathered, pos, sinks)
    mixed, outgoing = project(attended, all_o, resid[0], norm_gain, expert_ids[0])

    per_row = n_exp // SLICES
    members = [
        [
            (e // per_row) * n_exp + (e % per_row) * SLICES + 2 * rank + side
            for rank in range(2)
            for e in range(EXPERTS)
        ]
        for side in range(2)
    ]

    def exchange(value):
        return lax.all_to_all(
            value.reshape(2 * EXPERTS, 1, D),
            ("ctx", "exp"),
            0,
            0,
            tiled=True,
            axis_index_groups=members,
        ).reshape(2 * EXPERTS, D)

    arrived = exchange(outgoing)
    done = experts(arrived, mine + core + beside + core_beside)
    back = exchange(done)
    return combine(expert_ids[0], route_weights[0], mixed, back)[None]


def solution(mesh):
    return jax.shard_map(
        body,
        mesh=mesh,
        in_specs=(
            P("exp", "ctx", None),
            P("exp", "ctx", None, None),
            P("exp", "ctx"),
            P("exp", "ctx", None),
            P(),
            P("exp", None),
            P(),
            P("exp", "ctx", None),
            P("exp", "ctx", None),
            P(None, ("ctx", "exp")),
            P(None, ("ctx", "exp")),
            P(("ctx", "exp"), None),
        ),
        out_specs=P("exp", "ctx", None),
        check_vma=False,
    )
```
